32 devices in a mesh: groups: 2 (over x), seq: 16 (over z, y, core).
Axes of the slice: x: 2, y: 2, z: 4, core: 2. Of those that a mesh axis runs over, the one named last changes fastest.
Arguments:
- queries: bfloat16 [4096, 8192], P(('groups', 'seq')), parts along dimension 0, may hold values from -4.5 to 4.5
- keyvalue: bfloat16 [4096, 2048], P(('groups', 'seq')), parts along dimension 0, may hold values from -4.5 to 4.5
- doc_ids: int32 [4096], P(('groups', 'seq')), parts along dimension 0, may hold values from 0 to 7, never falling along the last dimension, each value on 1 to 512 neighbouring positions
- owner_tiles: int32 [32, 2], P(('groups', 'seq')), parts along dimension 0, may hold values from 0 to 15, as said below
- tile_counts: int32 [32], P(('groups', 'seq')), parts along dimension 0, may hold values from 0 to 2, as said below
Outputs:
- owned: bfloat16 [8192, 8192], P(('groups', 'seq')), parts along dimension 0
The draws below stay inside these ranges and needn't reach their ends.
There are 2 independent parts, one for each index of `groups`. The reference program is written for one: setup_inputs(seed, part) draws one part's arguments, and reference() takes and returns one part's arrays. A program takes and returns all parts, laid end to end along the dimension named above; each array names one. Nothing has to cross between parts.
Inputs may be any that keep to these rules, and one draw needn't show every extreme that they name: `owner_tiles`: over the slots below each owner's count, every tile 0 to 15 is listed exactly once; the other slots hold 0. Tile t is listed either by its holder, the owner o with o * 128 <= t * 128 < (o + 1) * 128, or by the holder's partner, the owner whose index differs from the holder's by half the number of owners. `tile_counts`: the counts sum to 16; each is 0, 1 or 2, some owner has 2, and an owner has 2 exactly when its partner has 0.
All inputs are finite; a program needn't handle non-finite values.
Results may differ from the reference program's by a relative error of at most 0.0034.
Values may be sent and summed in bfloat16 or wider, within the bound.
A program may use at most 64 MiB of HBM per device.

```python
import math
import jax
import jax.numpy as jnp
import numpy as np
from jax import lax

QUERY_HEADS = 64
KEY_VALUE_HEADS = 8
HEAD_WIDTH = 128
TILE = 128
DOCUMENT_LIMIT = 512
TOK_DEV = 128
SLAB_TOKENS = 2048
NTILE = 16
CAP = 2
DOCS = 8
N_SEQ = 16


def draw_queries(key, part):
    owner_key = jax.random.fold_in(key, 11)
    value_rows = jax.random.truncated_normal(owner_key, -4.0, 4.0, (SLAB_TOKENS, QUERY_HEADS, HEAD_WIDTH))
    return value_rows.astype(jnp.float32).reshape(SLAB_TOKENS, QUERY_HEADS * HEAD_WIDTH).astype(jnp.bfloat16)


def draw_keyvalue(key, part):
    owner_key = jax.random.fold_in(key, 23)
    value_rows = jax.random.truncated_normal(owner_key, -4.0, 4.0, (SLAB_TOKENS, KEY_VALUE_HEADS, 2, HEAD_WIDTH))
    return value_rows.astype(jnp.float32).reshape(SLAB_TOKENS, KEY_VALUE_HEADS * 2 * HEAD_WIDTH).astype(jnp.bfloat16)


def owner_plan(key):
    base = jax.random.fold_in(key, 5113)
    leading_entry, second, third, fourth = jax.random.split(base, 4)
    half = N_SEQ // 2
    per_device = TOK_DEV // TILE
    pair_rank = jnp.argsort(jax.random.permutation(leading_entry, half))
    movers = jax.random.randint(second, (), 1, half // 2 + 1)
    moving = pair_rank < movers
    side = jax.random.randint(third, (half,), 0, 2)
    devices = jnp.arange(N_SEQ, dtype=jnp.int32)
    pair = devices % half
    lower = devices < half
    moving_dev = moving[pair]
    giver = moving_dev & ((side[pair] == 0) == lower)
    taker = moving_dev & jnp.logical_not(giver)
    counts = jnp.where(giver, 0, jnp.where(taker, CAP, per_device)).astype(jnp.int32)
    local_tiles = jnp.arange(per_device, dtype=jnp.int32)
    own = devices[:, None] * per_device + local_tiles[None, :]
    partner = (devices + half) % N_SEQ
    theirs = partner[:, None] * per_device + local_tiles[None, :]
    candidates = jnp.concatenate([own, jnp.where(taker[:, None], theirs, 0)], axis=1)
    candidates = jnp.where(giver[:, None], 0, candidates)
    slots = jnp.arange(CAP, dtype=jnp.int32)
    shuffled = jax.random.permutation(fourth, jnp.tile(slots[None, :], (N_SEQ, 1)), axis=1, independent=True)
    scores = shuffled + jnp.where(slots[None, :] < counts[:, None], 0, CAP)
    order = jnp.argsort(scores, axis=1, stable=True)
    lists = jnp.take_along_axis(candidates, order, axis=1)
    lists = jnp.where(slots[None, :] < counts[:, None], lists, 0).astype(jnp.int32)
    return (lists, counts)


def draw_owner_tiles(key, part):
    lists, counts = owner_plan(key)
    return lists


def draw_tile_counts(key, part):
    lists, counts = owner_plan(key)
    return counts


def length_profile(count, total, most, lean):
    portions = [(1 << 20) // math.isqrt(standing ** lean) + 1 for standing in range(2, count + 1)]
    surplus, given = total - most - (count - 1), [1] * (count - 1)
    while surplus > 0:
        free = [i for i in range(count - 1) if given[i] < most]
        whole, left = sum([portions[i] for i in free]), surplus
        for i in free:
            addition = min(most - given[i], max(1, left * portions[i] // whole), surplus)
            given[i] = given[i] + addition
            surplus = surplus - addition
    return np.array([most] + given)


def ragged_sizes(key, number_of, total, most, slope):
    if number_of == 2:
        one = jax.random.randint(key, (), max(1, total - most), min(most, total - 1) + 1)
        return jnp.stack([one, total - one])
    lengths = jnp.asarray(length_profile(number_of, total, most, slope), jnp.int32)
    twos = (number_of - 1) // 2
    donor, taker = lengths[1:1 + 2 * twos:2], lengths[2:2 + 2 * twos:2]
    margin = jnp.minimum(donor - 1, most - taker)
    shifted = jax.random.randint(jax.random.fold_in(key, 1), (twos,), 0, 1 << 20) % (margin + 1)
    lengths = lengths.at[1:1 + 2 * twos:2].set(donor - shifted).at[2:2 + 2 * twos:2].set(taker + shifted)
    return lengths[jax.random.permutation(jax.random.fold_in(key, 2), number_of)]


def setup_inputs(seed: int = 0, part: int = 0) -> dict:
    arg_keys = jax.random.split(jax.random.key(seed), 6)
    part_splits = jax.random.split(jax.random.fold_in(arg_keys[5], part), 6)
    return {
        "queries": draw_queries(jax.random.fold_in(jax.random.fold_in(arg_keys[5], part), 71), part),
        "keyvalue": draw_keyvalue(jax.random.fold_in(jax.random.fold_in(arg_keys[5], part), 71), part),
        "doc_ids": jnp.searchsorted(jnp.cumsum(ragged_sizes(part_splits[2], DOCS, SLAB_TOKENS, DOCUMENT_LIMIT, 2)), jnp.arange(SLAB_TOKENS), side="right").astype(jnp.int32),
        "owner_tiles": draw_owner_tiles(jax.random.fold_in(jax.random.fold_in(arg_keys[5], part), 71), part),
        "tile_counts": draw_tile_counts(jax.random.fold_in(jax.random.fold_in(arg_keys[5], part), 71), part),
    }


def attend(queries, keys, value_rows, allowed):
    scale = HEAD_WIDTH ** -0.5
    scores = jnp.einsum("rhgd,khd->hgrk", queries.astype(jnp.float32), keys.astype(jnp.float32)) * scale
    scores = jnp.where(allowed[None, None], scores, -jnp.inf)
    row_top = jnp.max(scores, axis=3, keepdims=True)
    exponent = jnp.exp(scores - row_top)
    totals = jnp.sum(exponent, axis=3, keepdims=True)
    weights = exponent.astype(jnp.bfloat16)
    mixed_rows = jnp.einsum("hgrk,khd->rhgd", weights.astype(jnp.float32), value_rows.astype(jnp.float32))
    return (mixed_rows / jnp.transpose(totals, (2, 0, 1, 3))).astype(jnp.bfloat16)


def reference(queries, keyvalue, doc_ids, owner_tiles, tile_counts):
    group_width = QUERY_HEADS // KEY_VALUE_HEADS
    row_block = min(512, SLAB_TOKENS)
    query_heads = queries.reshape(SLAB_TOKENS, KEY_VALUE_HEADS, group_width, HEAD_WIDTH)
    keyvalue_heads = keyvalue.reshape(SLAB_TOKENS, KEY_VALUE_HEADS, 2, HEAD_WIDTH)
    padded_extent = jnp.zeros((DOCUMENT_LIMIT, KEY_VALUE_HEADS, 2, HEAD_WIDTH), keyvalue.dtype)
    kv_pad = jnp.concatenate([padded_extent, keyvalue_heads], axis=0)
    docs_pad = jnp.concatenate([jnp.full((DOCUMENT_LIMIT,), -1, jnp.int32), doc_ids.astype(jnp.int32)], axis=0)

    def one_block(block_id):
        begin_row = block_id * row_block
        q_block = lax.dynamic_slice_in_dim(query_heads, begin_row, row_block, 0)
        kv_block = lax.dynamic_slice_in_dim(kv_pad, begin_row, row_block + DOCUMENT_LIMIT, 0)
        q_docs = lax.dynamic_slice_in_dim(doc_ids.astype(jnp.int32), begin_row, row_block, 0)
        k_docs = lax.dynamic_slice_in_dim(docs_pad, begin_row, row_block + DOCUMENT_LIMIT, 0)
        q_place = jnp.arange(row_block, dtype=jnp.int32) + DOCUMENT_LIMIT
        k_place = jnp.arange(row_block + DOCUMENT_LIMIT, dtype=jnp.int32)
        allowed = (q_docs[:, None] == k_docs[None, :]) & (k_place[None, :] <= q_place[:, None])
        result = attend(q_block, kv_block[:, :, 0], kv_block[:, :, 1], allowed)
        return result.reshape(row_block, QUERY_HEADS * HEAD_WIDTH)

    attended = lax.map(one_block, jnp.arange(SLAB_TOKENS // row_block, dtype=jnp.int32)).reshape(SLAB_TOKENS, QUERY_HEADS * HEAD_WIDTH)
    tiles = attended.reshape(NTILE, TILE, QUERY_HEADS * HEAD_WIDTH)
    picked = jnp.take(tiles, owner_tiles.reshape(-1).astype(jnp.int32), axis=0)
    live = (jnp.arange(CAP, dtype=jnp.int32)[None, :] < tile_counts[:, None]).reshape(-1)
    owned = jnp.where(live[:, None, None], picked, jnp.zeros((), attended.dtype))
    return owned.reshape(N_SEQ * CAP * TILE, QUERY_HEADS * HEAD_WIDTH)
```

```python
import jax
import jax.numpy as jnp
from jax import lax
from jax.sharding import PartitionSpec as P

QUERY_HEADS = 64
KEY_VALUE_HEADS = 8
HEAD_WIDTH = 128
TILE = 128
DOCUMENT_LIMIT = 512


def from_behind(shard, axis, by):
    count = lax.axis_size(axis)
    pairs = [(i, i + by) for i in range(count) if 0 <= i + by < count]
    return lax.ppermute(shard, axis, pairs)


def attend(queries, keys, value_rows, allowed):
    scale = queries.shape[-1] ** (-0.5)
    scores = jnp.einsum("rhgd,khd->hgrk", queries, keys, preferred_element_type=jnp.float32) * scale
    scores = jnp.where(allowed[None, None], scores, -jnp.inf)
    row_top = jnp.max(scores, axis=3, keepdims=True)
    exponent = jnp.exp(scores - row_top)
    totals = jnp.sum(exponent, axis=3, keepdims=True)
    weights = exponent.astype(jnp.bfloat16)
    mixed_rows = jnp.einsum(
        "hgrk,khd->rhgd", weights, value_rows, preferred_element_type=jnp.float32
    )
    return (mixed_rows / jnp.transpose(totals, (2, 0, 1, 3))).astype(jnp.bfloat16)


def local(queries, keyvalue, doc_ids, owner_tiles, tile_counts):
    seq_count = lax.axis_size("seq")
    token_per_holder = queries.shape[0]
    width = queries.shape[1]
    group_width = QUERY_HEADS // KEY_VALUE_HEADS
    slots_dev = owner_tiles.shape[1]
    reach_devs = (DOCUMENT_LIMIT - 1) // token_per_holder + 1
    doc_marks = doc_ids + 1
    kv_parts = [keyvalue]
    mark_parts = [doc_marks]
    for shift_by in range(1, reach_devs + 1):
        far_kv, far_marks = from_behind((keyvalue, doc_marks), "seq", shift_by)
        kv_parts.insert(0, far_kv)
        mark_parts.insert(0, far_marks)
    kv_near = jnp.concatenate(kv_parts, axis=0)
    near_marks = jnp.concatenate(mark_parts, axis=0)
    near_rows = kv_near.shape[0]
    keyvalue_grouped = kv_near.reshape(near_rows, KEY_VALUE_HEADS, 2, HEAD_WIDTH)
    q_place = jnp.arange(token_per_holder, dtype=jnp.int32) + reach_devs * token_per_holder
    k_place = jnp.arange(near_rows, dtype=jnp.int32)
    allowed = (doc_marks[:, None] == near_marks[None, :]) & (k_place[None, :] <= q_place[:, None])
    local_out = attend(
        queries.reshape(token_per_holder, KEY_VALUE_HEADS, group_width, HEAD_WIDTH),
        keyvalue_grouped[:, :, 0],
        keyvalue_grouped[:, :, 1],
        allowed,
    )
    local_out = local_out.reshape(token_per_holder, width)
    half = seq_count // 2
    swap = [(i, (i + half) % seq_count) for i in range(seq_count)]
    far_out = lax.ppermute(local_out, "seq", swap)
    me = lax.axis_index("seq")
    live = jnp.arange(slots_dev, dtype=jnp.int32) < tile_counts[0]
    mine = (owner_tiles[0] == me)[:, None, None]
    owned = jnp.where(mine, local_out[None], far_out[None])
    owned = jnp.where(live[:, None, None], owned, jnp.zeros((), jnp.bfloat16))
    return owned.reshape(slots_dev * TILE, width)


def solution(mesh):
    placed = (
        P(("groups", "seq"), None),
        P(("groups", "seq"), None),
        P(("groups", "seq")),
        P(("groups", "seq"), None),
        P(("groups", "seq")),
    )
    return jax.shard_map(
        local, mesh=mesh, in_specs=placed, out_specs=P(("groups", "seq"), None), check_vma=False
    )
```

```python
import functools

import jax
import jax.numpy as jnp
from jax import lax
from jax.experimental import pallas as pl
from jax.experimental.pallas import tpu as pltpu
from jax.sharding import PartitionSpec as P

QUERY_HEADS = 64
KEY_VALUE_HEADS = 8
HEAD_WIDTH = 128
TILE = 128
DOCUMENT_LIMIT = 512

MESH = pl.DeviceIdType.MESH
NEAR_TILES = DOCUMENT_LIMIT // TILE + 1
GROUP_HEADS = QUERY_HEADS // KEY_VALUE_HEADS
HALF_HEADS = GROUP_HEADS // 2
HALF_COLS = HALF_HEADS * HEAD_WIDTH
KV_COLS = 2 * HEAD_WIDTH
MASKED = -1e30
VMEM = pl.BlockSpec(memory_space=pltpu.VMEM)


class Place:
    def __init__(self, count):
        self.me = me = lax.axis_index("seq")
        self.core = lax.rem(me, 2)
        self.chip = chip = lax.div(me, 2)
        self.line = lax.rem(chip, 2)
        self.depth = lax.div(chip, 2)
        self.depths = count // 4
        reach = self.depths // 2
        self.low = self.depth < reach
        step = jnp.where(self.low, 4, -4)
        self.inner = me + step
        self.outer = me - step
        self.rim = jnp.where(self.low, self.depth, self.depths - 1 - self.depth)
        self.crossing = self.rim == reach - 1
        self.sibling = me + 1 - 2 * self.core


def remote(src, dst, send_sem, recv_sem, seq):
    return pltpu.make_async_remote_copy(
        src_ref=src, dst_ref=dst, send_sem=send_sem, recv_sem=recv_sem,
        device_id={"seq": seq}, device_id_type=MESH)


class Bus:
    def __init__(self, at, o, plan, sib, far, farsib, injin, inj, sends, recvs, turn):
        self.__dict__.update(locals())

    def share(self, h):
        return remote(self.o.at[h, 1 - self.at.core], self.sib.at[h],
                      self.sends.at[0, h], self.recvs.at[0, h], self.at.sibling)

    def inward(self, h):
        return remote(self.inj.at[h], self.injin.at[h],
                      self.sends.at[1, h], self.recvs.at[1, h], self.at.inner)

    def across(self, h):
        return remote(self.inj.at[h], self.far.at[h],
                      self.sends.at[1, h], self.recvs.at[2, h], self.at.inner)

    def outward(self, h):
        return remote(self.far.at[h], self.far.at[h],
                      self.sends.at[2, h], self.recvs.at[2, h], self.at.outer)

    def hand(self, h):
        return remote(self.far.at[h], self.farsib.at[h],
                      self.sends.at[3, h], self.recvs.at[3, h], self.at.sibling)

    def compose(self, h, below):
        turn = self.turn()
        own_here = jnp.broadcast_to(self.plan[0:1, :] == turn, (TILE, TILE))
        sib_here = jnp.broadcast_to(self.plan[8:9, :] == turn, (TILE, TILE))
        for c in range(0, HALF_COLS, TILE):
            cols = slice(c, c + TILE)
            own = self.o[h, self.at.core, :, cols].astype(jnp.float32)
            new = self.sib[h, :, cols].astype(jnp.float32)
            if below:
                new = jnp.where(sib_here, new, self.injin[h, :, cols].astype(jnp.float32))
            self.inj[h, :, cols] = jnp.where(own_here, own, new).astype(jnp.bfloat16)

    def inject(self, h, shared=True):
        if shared:
            self.share(h).wait_recv()

        @pl.when(self.at.rim == 0)
        def _():
            self.compose(h, False)

        @pl.when(self.at.rim > 0)
        def _():
            self.inward(h).wait_recv()
            self.compose(h, True)

        @pl.when(self.at.crossing)
        def _():
            self.across(h).start()

        @pl.when(jnp.logical_not(self.at.crossing))
        def _():
            self.inward(h).start()

    def forward(self, h):
        self.outward(h).wait_recv()

        @pl.when(self.at.rim > 0)
        def _():
            self.outward(h).start()

        self.hand(h).start()

    def drain(self, h, shared=True):
        if shared:
            self.share(h).wait_send()
        self.inward(h).wait_send()

        @pl.when(self.at.rim > 0)
        def _():
            self.outward(h).wait_send()

        self.hand(h).wait()


def main_kernel(groups, count, kv_hbm, q, qmark, info,
                o, sib, far, farsib, plan, top,
                kv, ginfo, bias, injin, inj, topin,
                kvl, info_s, info_r, top_s, top_r, kv_s, kv_r, bus_s, bus_r):
    at = Place(count)
    me, core, chip, line = at.me, at.core, at.chip, at.line
    group = lax.axis_index("groups")
    chips = count // 2
    bus = Bus(at, o, plan, sib, far, farsib, injin, inj, bus_s, bus_r, lambda: 0)

    def own(h):
        return kv_hbm.at[:, pl.ds(pl.multiple_of(h * KV_COLS, KV_COLS), KV_COLS)]

    def local(h):
        return pltpu.make_async_copy(own(h), kv.at[h, 4 + core], kvl.at[h])

    def up_two(h):
        return remote(own(h), kv.at[h, core], kv_s.at[0, h], kv_r.at[h, core], me + 4)

    def up_one(h):
        return remote(own(h), kv.at[h, 2 + core], kv_s.at[1, h], kv_r.at[h, 2 + core], me + 2)

    def relay_one(h):
        return remote(kv.at[h, core], kv.at[h, 2 + core], kv_s.at[1, h], kv_r.at[h, 2 + core], me - 2)

    def sib_own(h):
        return remote(own(h), kv.at[h, 4], kv_s.at[2, h], kv_r.at[h, 4], at.sibling)

    def sib_one(h):
        return remote(kv.at[h, 2 + core], kv.at[h, 2 + core], kv_s.at[3, h],
                      kv_r.at[h, 2 + core], at.sibling)

    def sib_two(h):
        return remote(kv.at[h, 1], kv.at[h, 1], kv_s.at[4, h], kv_r.at[h, 1], at.sibling)

    def arrived(h, slot):
        remote(kv.at[h, slot], kv.at[h, slot], kv_s.at[0, h], kv_r.at[h, slot],
               at.sibling).wait_recv()

    def info_to(peer):
        return remote(info, ginfo.at[me], info_s.at[peer], info_r.at[me], peer)

    def info_from(peer):
        return remote(info, ginfo.at[peer], info_s.at[peer], info_r.at[peer], peer)

    def top_copy(by):
        to = lax.rem(group + by, groups)
        return pltpu.make_async_remote_copy(
            src_ref=top, dst_ref=topin.at[by], send_sem=top_s.at[by], recv_sem=top_r.at[by],
            device_id={"groups": to}, device_id_type=MESH)

    def each(n, body):
        lax.fori_loop(0, n, lambda i, c: (body(i), c)[1], 0)

    def peers(body):
        def one(i):
            body(lax.rem(me + 1 + i, count))
        each(count - 1, one)

    heads = functools.partial(each, KEY_VALUE_HEADS)

    heads(lambda h: local(h).start())
    barrier = pltpu.get_barrier_semaphore()
    peers(lambda p: pl.semaphore_signal(barrier, inc=1, device_id={"seq": p}, device_id_type=MESH))
    for by in range(1, groups):
        pl.semaphore_signal(barrier, inc=1, device_id={"groups": lax.rem(group + by, groups)},
                            device_id_type=MESH)
    pl.semaphore_wait(barrier, count - 1 + groups - 1)

    has_two_up = chip + 2 < chips

    def launch(h):
        @pl.when(has_two_up)
        def _():
            up_two(h).start()

        @pl.when(line == 0)
        def _():
            up_one(h).start()

        @pl.when(core == 0)
        def _():
            sib_own(h).start()

    launch(0)
    peers(lambda p: info_to(p).start())
    each(KEY_VALUE_HEADS - 1, lambda h: launch(h + 1))

    blank = jnp.zeros((TILE, KV_COLS), jnp.bfloat16)

    @pl.when(chip < 2)
    def _():
        def clear(h):
            kv[h, 0] = blank
            kv[h, 1] = blank
        heads(clear)

    @pl.when(chip < 1)
    def _():
        def clear(h):
            kv[h, 2] = blank
            kv[h, 3] = blank
        heads(clear)

    ginfo[me] = info[...]
    peers(lambda p: info_from(p).wait_recv())

    rows = lax.broadcasted_iota(jnp.int32, (TILE, TILE), 0)
    cols = lax.broadcasted_iota(jnp.int32, (TILE, TILE), 1)
    for w in range(NEAR_TILES):
        tile = me - (NEAR_TILES - 1) + w
        marks = ginfo[jnp.maximum(tile, 0), 0:1, :] - jnp.where(tile < 0, 1 << 20, 0)
        allowed = qmark[...] == jnp.broadcast_to(marks, (TILE, TILE))
        if w == NEAR_TILES - 1:
            allowed = allowed & (cols <= rows)
        bias[:, w * TILE:(w + 1) * TILE] = jnp.where(allowed, 0.0, MASKED).astype(jnp.float32)

    partner = lax.rem(me + count // 2, count)
    reach = at.depths // 2

    def tally(i, carry):
        ahead_me, ahead_sib, ahead_far, totals = carry
        gives = jnp.where(ginfo[i, 8:16, :] == 0, 1, 0)
        ichip = lax.div(i, 2)
        iline = lax.rem(ichip, 2)
        ilow = lax.div(ichip, 2) < reach
        here = jnp.where((iline == line) & (ilow == at.low), 1, 0)
        there = jnp.where((iline == line) & (ilow != at.low), 1, 0)
        ahead_me = ahead_me + gives * (here * jnp.where(i < me, 1, 0))
        ahead_sib = ahead_sib + gives * (here * jnp.where(i < at.sibling, 1, 0))
        ahead_far = ahead_far + gives * (there * jnp.where(i < partner, 1, 0))
        totals = tuple(
            t + gives * jnp.where((iline == b % 2) & (jnp.where(ilow, 1, 0) == b // 2), 1, 0)
            for b, t in enumerate(totals))
        return ahead_me, ahead_sib, ahead_far, totals

    zero = jnp.zeros((8, TILE), jnp.int32)
    ahead_me, ahead_sib, ahead_far, totals = lax.fori_loop(
        0, count, tally, (zero, zero, zero, (zero,) * 4))
    for slot, (who, ahead) in enumerate(((me, ahead_me), (at.sibling, ahead_sib), (partner, ahead_far))):
        plan[slot * 8:slot * 8 + 8, :] = jnp.where(ginfo[who, 8:16, :] == 0, ahead, -1)
    top[...] = jnp.maximum(jnp.maximum(totals[0], totals[1]), jnp.maximum(totals[2], totals[3]))

    scale = HEAD_WIDTH ** -0.5

    def attend(h):
        def half(k, c):
            keys = kv[h, pl.ds(core, NEAR_TILES), :, 0:HEAD_WIDTH].reshape(NEAR_TILES * TILE, HEAD_WIDTH)
            vals = kv[h, pl.ds(core, NEAR_TILES), :, HEAD_WIDTH:].reshape(NEAR_TILES * TILE, HEAD_WIDTH)
            for j in range(HALF_HEADS):
                at_col = pl.multiple_of((h * GROUP_HEADS + k * HALF_HEADS + j) * HEAD_WIDTH, HEAD_WIDTH)
                s = lax.dot_general(q[:, pl.ds(at_col, HEAD_WIDTH)], keys, (((1,), (1,)), ((), ())),
                                    preferred_element_type=jnp.float32)
                s = s * scale + bias[...]
                e = jnp.exp(s - jnp.max(s, axis=1, keepdims=True))
                total = jnp.sum(e, axis=1, keepdims=True)
                mixed = jnp.dot(e.astype(jnp.bfloat16), vals, preferred_element_type=jnp.float32)
                o[h, k, :, j * HEAD_WIDTH:(j + 1) * HEAD_WIDTH] = (mixed / total).astype(jnp.bfloat16)
            return c
        lax.fori_loop(0, 2, half, 0)

    def relay_two(h):
        @pl.when(chip >= 2)
        def _():
            arrived(h, core)

            @pl.when(line == 1)
            def _():
                relay_one(h).start()

            @pl.when(core == 1)
            def _():
                sib_two(h).start()

    def relay_sib(h):
        @pl.when(chip >= 1)
        def _():
            arrived(h, 2 + core)
            sib_one(h).start()

    def compute(h):
        @pl.when(chip >= 1)
        def _():
            arrived(h, 3 - core)

        @pl.when((chip >= 2) & (core == 0))
        def _():
            arrived(h, 1)

        @pl.when(core == 1)
        def _():
            arrived(h, 4)

        local(h).wait()
        attend(h)
        bus.share(h).start()

    def step(u):
        for lag, stage in ((0, relay_two), (1, relay_sib), (2, compute), (3, bus.inject), (5, bus.forward)):
            h = u - lag

            @pl.when((h >= 0) & (h < KEY_VALUE_HEADS))
            def _():
                stage(h)

    each(KEY_VALUE_HEADS + 5, step)

    for by in range(1, groups):
        top_copy(by).start()

    def drain(h):
        bus.drain(h)

        @pl.when(has_two_up)
        def _():
            up_two(h).wait_send()

        @pl.when((line == 0) | (chip >= 2))
        def _():
            up_one(h).wait_send()

        @pl.when(core == 0)
        def _():
            sib_own(h).wait_send()

        @pl.when(chip >= 1)
        def _():
            sib_one(h).wait_send()

        @pl.when((chip >= 2) & (core == 1))
        def _():
            sib_two(h).wait_send()

    heads(drain)
    peers(lambda p: info_to(p).wait_send())
    for by in range(1, groups):
        top_copy(by).wait()
    most = top[...]
    for by in range(1, groups):
        most = jnp.maximum(most, topin[by])
    top[...] = most


def round_kernel(count, o, sib, plan, turn, far, farsib, injin, inj, bus_s, bus_r):
    at = Place(count)
    barrier = pltpu.get_barrier_semaphore()
    for seq, there in ((at.sibling, None), (at.inner, None), (at.outer, at.rim > 0)):
        def greet():
            pl.semaphore_signal(barrier, inc=1, device_id={"seq": seq}, device_id_type=MESH)
        if there is None:
            greet()
        else:
            pl.when(there)(greet)
    pl.semaphore_wait(barrier, jnp.where(at.rim > 0, 3, 2))

    bus = Bus(at, o, plan, sib, far, farsib, injin, inj, bus_s, bus_r, lambda: turn[0:1, :])

    def step(u, c):
        for lag, stage in ((0, functools.partial(bus.inject, shared=False)), (2, bus.forward)):
            h = u - lag

            @pl.when((h >= 0) & (h < KEY_VALUE_HEADS))
            def _():
                stage(h)
        return c

    lax.fori_loop(0, KEY_VALUE_HEADS + 2, step, 0)

    def drain(h, c):
        bus.drain(h, shared=False)
        return c

    lax.fori_loop(0, KEY_VALUE_HEADS, drain, 0)


def place_kernel(facts, o, far, farsib, out):
    k = lax.rem(pl.program_id(0), 2)
    slots = out.shape[0] // TILE
    me, core, valid = facts[slots], facts[slots + 1], facts[slots + 2]
    for s in range(slots):
        live, mine = s < valid, facts[s] == me
        rows = slice(s * TILE, (s + 1) * TILE)

        @pl.when(live & mine)
        def _():
            out[rows, :] = o[0, 0]

        @pl.when(live & jnp.logical_not(mine) & (k == core))
        def _():
            out[rows, :] = far[0]

        @pl.when(live & jnp.logical_not(mine) & (k != core))
        def _():
            out[rows, :] = farsib[0]

        @pl.when(jnp.logical_not(live))
        def _():
            out[rows, :] = jnp.zeros((TILE, HALF_COLS), jnp.bfloat16)


def local(groups, count, queries, keyvalue, doc_ids, owner_tiles, tile_counts):
    width = queries.shape[1]
    slots = owner_tiles.shape[1]
    marks = doc_ids + 1
    info = jnp.concatenate([
        jnp.broadcast_to(marks[None, :], (8, TILE)),
        jnp.broadcast_to(tile_counts[:, None], (8, TILE))], axis=0)
    qmark = jnp.broadcast_to(marks[:, None], (TILE, TILE))
    H = KEY_VALUE_HEADS
    bf, i32 = jnp.bfloat16, jnp.int32
    part = (H, TILE, HALF_COLS)
    dma = pltpu.SemaphoreType.DMA
    o, sib, far, farsib, plan, top = pl.pallas_call(
        functools.partial(main_kernel, groups, count),
        out_shape=[
            jax.ShapeDtypeStruct((H, 2, TILE, HALF_COLS), bf),
            jax.ShapeDtypeStruct(part, bf),
            jax.ShapeDtypeStruct(part, bf),
            jax.ShapeDtypeStruct(part, bf),
            jax.ShapeDtypeStruct((24, TILE), i32),
            jax.ShapeDtypeStruct((8, TILE), i32),
        ],
        in_specs=[pl.BlockSpec(memory_space=pl.ANY), VMEM, VMEM, VMEM],
        out_specs=[VMEM] * 6,
        scratch_shapes=[
            pltpu.VMEM((H, 6, TILE, KV_COLS), bf),
            pltpu.VMEM((count, 16, TILE), i32),
            pltpu.VMEM((TILE, NEAR_TILES * TILE), jnp.float32),
            pltpu.VMEM(part, bf),
            pltpu.VMEM(part, bf),
            pltpu.VMEM((groups, 8, TILE), i32),
            dma((H,)),
            dma((count,)),
            dma((count,)),
            dma((groups,)),
            dma((groups,)),
            dma((5, H)),
            dma((H, 6)),
            dma((4, H)),
            dma((4, H)),
        ],
        compiler_params=pltpu.CompilerParams(
            collective_id=0, has_side_effects=True, vmem_limit_bytes=40 << 20),
    )(keyvalue, queries, qmark, info)

    def again(turn, held):
        turns = jnp.full((8, TILE), turn, i32)
        new = pl.pallas_call(
            functools.partial(round_kernel, count),
            out_shape=[jax.ShapeDtypeStruct(part, bf)] * 2,
            in_specs=[VMEM] * 4,
            out_specs=[VMEM] * 2,
            scratch_shapes=[
                pltpu.VMEM(part, bf),
                pltpu.VMEM(part, bf),
                dma((4, H)),
                dma((4, H)),
            ],
            compiler_params=pltpu.CompilerParams(
                collective_id=1, has_side_effects=True, vmem_limit_bytes=24 << 20),
        )(o, sib, plan, turns)
        here = plan[16, 0] == turn
        return tuple(jnp.where(here, n, h) for n, h in zip(new, held))

    far, farsib = lax.fori_loop(1, top[0, 0], again, (far, farsib))

    me = lax.axis_index("seq")
    facts = jnp.concatenate([owner_tiles[0], jnp.stack([me, lax.rem(me, 2), tile_counts[0]])])
    return pl.pallas_call(
        place_kernel,
        grid=(2 * H,),
        out_shape=jax.ShapeDtypeStruct((slots * TILE, width), bf),
        in_specs=[
            pl.BlockSpec(memory_space=pltpu.SMEM),
            pl.BlockSpec((1, 1, TILE, HALF_COLS), lambda i: (i // 2, i % 2, 0, 0)),
            pl.BlockSpec((1, TILE, HALF_COLS), lambda i: (i // 2, 0, 0)),
            pl.BlockSpec((1, TILE, HALF_COLS), lambda i: (i // 2, 0, 0)),
        ],
        out_specs=pl.BlockSpec((slots * TILE, HALF_COLS), lambda i: (0, i)),
    )(facts, o, far, farsib)


def solution(mesh):
    spread = P(("groups", "seq"))
    rows = P(("groups", "seq"), None)
    return jax.shard_map(
        functools.partial(local, mesh.shape["groups"], mesh.shape["seq"]), mesh=mesh,
        in_specs=(rows, rows, spread, rows, spread), out_specs=rows, check_vma=False)
```

```python
import functools

import jax
import jax.numpy as jnp
from jax import lax
from jax.experimental import pallas as pl
from jax.experimental.pallas import tpu as pltpu
from jax.sharding import PartitionSpec as P

QUERY_HEADS = 64
KEY_VALUE_HEADS = 8
HEAD_WIDTH = 128
TILE = 128
DOCUMENT_LIMIT = 512

MESH = pl.DeviceIdType.MESH
NEAR_TILES = DOCUMENT_LIMIT // TILE + 1
GROUP_HEADS = QUERY_HEADS // KEY_VALUE_HEADS
HALF_HEADS = GROUP_HEADS // 2
HALF_COLS = HALF_HEADS * HEAD_WIDTH
GROUP_COLS = 2 * HALF_COLS
KV_COLS = 2 * HEAD_WIDTH
MASKED = -1e30
VMEM = pl.BlockSpec(memory_space=pltpu.VMEM)


class Place:
    def __init__(self, count):
        self.me = me = lax.axis_index("seq")
        self.core = lax.rem(me, 2)
        self.chip = chip = lax.div(me, 2)
        self.line = lax.rem(chip, 2)
        self.depth = lax.div(chip, 2)
        self.depths = count // 4
        reach = self.depths // 2
        self.low = self.depth < reach
        step = jnp.where(self.low, 4, -4)
        self.inner = me + step
        self.outer = me - step
        self.rim = jnp.where(self.low, self.depth, self.depths - 1 - self.depth)
        self.crossing = self.rim == reach - 1
        self.lag = 2 * (2 * (reach - 1 - self.rim) + 1)
        self.longest = 2 * (2 * reach - 1)
        self.sibling = me + 1 - 2 * self.core


def remote(src, dst, send_sem, recv_sem, seq):
    return pltpu.make_async_remote_copy(
        src_ref=src, dst_ref=dst, send_sem=send_sem, recv_sem=recv_sem,
        device_id={"seq": seq}, device_id_type=MESH)


class Bus:
    def __init__(self, at, o, plan, sib, far, farsib, injin, inj, sends, recvs, turn):
        self.__dict__.update(locals())

    def share(self, h):
        return remote(self.o.at[h, 1 - self.at.core], self.sib.at[h],
                      self.sends.at[0, h], self.recvs.at[0, h], self.at.sibling)

    def inward(self, h):
        return remote(self.inj.at[h], self.injin.at[h],
                      self.sends.at[1, h], self.recvs.at[1, h], self.at.inner)

    def across(self, h):
        return remote(self.inj.at[h], self.far.at[h],
                      self.sends.at[1, h], self.recvs.at[2, h], self.at.inner)

    def outward(self, h):
        return remote(self.far.at[h], self.far.at[h],
                      self.sends.at[2, h], self.recvs.at[2, h], self.at.outer)

    def hand(self, h):
        return remote(self.far.at[h], self.farsib.at[h],
                      self.sends.at[3, h], self.recvs.at[3, h], self.at.sibling)

    def compose(self, h, below):
        turn = self.turn()
        own_here = jnp.broadcast_to(self.plan[0:1, :] == turn, (TILE, TILE))
        sib_here = jnp.broadcast_to(self.plan[8:9, :] == turn, (TILE, TILE))
        for c in range(0, HALF_COLS, TILE):
            cols = slice(c, c + TILE)
            own = self.o[h, self.at.core, :, cols].astype(jnp.float32)
            new = self.sib[h, :, cols].astype(jnp.float32)
            if below:
                new = jnp.where(sib_here, new, self.injin[h, :, cols].astype(jnp.float32))
            self.inj[h, :, cols] = jnp.where(own_here, own, new).astype(jnp.bfloat16)

    def inject(self, h, shared=True):
        if shared:
            self.share(h).wait_recv()

        @pl.when(self.at.rim == 0)
        def _():
            self.compose(h, False)

        @pl.when(self.at.rim > 0)
        def _():
            self.inward(h).wait_recv()
            self.compose(h, True)

        @pl.when(self.at.crossing)
        def _():
            self.across(h).start()

        @pl.when(jnp.logical_not(self.at.crossing))
        def _():
            self.inward(h).start()

    def forward(self, h):
        self.outward(h).wait_recv()

        @pl.when(self.at.rim > 0)
        def _():
            self.outward(h).start()

        self.hand(h).start()

    def drain(self, h, shared=True):
        if shared:
            self.share(h).wait_send()
        self.inward(h).wait_send()

        @pl.when(self.at.rim > 0)
        def _():
            self.outward(h).wait_send()

        self.hand(h).wait()


def main_kernel(groups, count, kv_hbm, q_hbm, qmark, info,
                o, sib, far, farsib, plan, top,
                q, kv, ginfo, bias, injin, inj, topin,
                ql, kvl, info_s, info_r, top_s, top_r, kv_s, kv_r, bus_s, bus_r):
    at = Place(count)
    me, core, chip, line = at.me, at.core, at.chip, at.line
    group = lax.axis_index("groups")
    chips = count // 2
    bus = Bus(at, o, plan, sib, far, farsib, injin, inj, bus_s, bus_r, lambda: 0)

    def own(h):
        return kv_hbm.at[:, pl.ds(pl.multiple_of(h * KV_COLS, KV_COLS), KV_COLS)]

    def local(h):
        return pltpu.make_async_copy(own(h), kv.at[h, 4 + core], kvl.at[h])

    def q_copy(h):
        cols = pl.ds(pl.multiple_of(h * GROUP_COLS, GROUP_COLS), GROUP_COLS)
        return pltpu.make_async_copy(q_hbm.at[:, cols], q.at[:, cols], ql.at[h])

    def up_two(h):
        return remote(own(h), kv.at[h, core], kv_s.at[0, h], kv_r.at[h, core], me + 4)

    def up_one(h):
        return remote(own(h), kv.at[h, 2 + core], kv_s.at[1, h], kv_r.at[h, 2 + core], me + 2)

    def relay_one(h):
        return remote(kv.at[h, core], kv.at[h, 2 + core], kv_s.at[1, h], kv_r.at[h, 2 + core], me - 2)

    def sib_own(h):
        return remote(own(h), kv.at[h, 4], kv_s.at[2, h], kv_r.at[h, 4], at.sibling)

    def sib_one(h):
        return remote(kv.at[h, 2 + core], kv.at[h, 2 + core], kv_s.at[3, h],
                      kv_r.at[h, 2 + core], at.sibling)

    def sib_two(h):
        return remote(kv.at[h, 1], kv.at[h, 1], kv_s.at[4, h], kv_r.at[h, 1], at.sibling)

    def arrived(h, slot):
        remote(kv.at[h, slot], kv.at[h, slot], kv_s.at[0, h], kv_r.at[h, slot],
               at.sibling).wait_recv()

    def info_to(peer):
        return remote(info, ginfo.at[me], info_s.at[peer], info_r.at[me], peer)

    def info_from(peer):
        return remote(info, ginfo.at[peer], info_s.at[peer], info_r.at[peer], peer)

    def top_copy(by):
        to = lax.rem(group + by, groups)
        return pltpu.make_async_remote_copy(
            src_ref=top, dst_ref=topin.at[by], send_sem=top_s.at[by], recv_sem=top_r.at[by],
            device_id={"groups": to}, device_id_type=MESH)

    def each(n, body):
        lax.fori_loop(0, n, lambda i, c: (body(i), c)[1], 0)

    def peers(body):
        def one(i):
            body(lax.rem(me + 1 + i, count))
        each(count - 1, one)

    heads = functools.partial(each, KEY_VALUE_HEADS)

    heads(lambda h: local(h).start())
    heads(lambda h: q_copy(h).start())
    barrier = pltpu.get_barrier_semaphore()
    peers(lambda p: pl.semaphore_signal(barrier, inc=1, device_id={"seq": p}, device_id_type=MESH))
    for by in range(1, groups):
        pl.semaphore_signal(barrier, inc=1, device_id={"groups": lax.rem(group + by, groups)},
                            device_id_type=MESH)
    pl.semaphore_wait(barrier, count - 1 + groups - 1)

    has_two_up = chip + 2 < chips

    def launch(h):
        @pl.when(has_two_up)
        def _():
            up_two(h).start()

        @pl.when(line == 0)
        def _():
            up_one(h).start()

        @pl.when(core == 0)
        def _():
            sib_own(h).start()

    launch(0)
    peers(lambda p: info_to(p).start())
    each(KEY_VALUE_HEADS - 1, lambda h: launch(h + 1))

    blank = jnp.zeros((TILE, KV_COLS), jnp.bfloat16)

    @pl.when(chip < 2)
    def _():
        def clear(h):
            kv[h, 0] = blank
            kv[h, 1] = blank
        heads(clear)

    @pl.when(chip < 1)
    def _():
        def clear(h):
            kv[h, 2] = blank
            kv[h, 3] = blank
        heads(clear)

    ginfo[me] = info[...]
    peers(lambda p: info_from(p).wait_recv())

    rows = lax.broadcasted_iota(jnp.int32, (TILE, TILE), 0)
    cols = lax.broadcasted_iota(jnp.int32, (TILE, TILE), 1)
    for w in range(NEAR_TILES):
        tile = me - (NEAR_TILES - 1) + w
        marks = ginfo[jnp.maximum(tile, 0), 0:1, :] - jnp.where(tile < 0, 1 << 20, 0)
        allowed = qmark[...] == jnp.broadcast_to(marks, (TILE, TILE))
        if w == NEAR_TILES - 1:
            allowed = allowed & (cols <= rows)
        bias[:, w * TILE:(w + 1) * TILE] = jnp.where(allowed, 0.0, MASKED).astype(jnp.float32)

    partner = lax.rem(me + count // 2, count)
    reach = at.depths // 2

    def tally(i, carry):
        ahead_me, ahead_sib, ahead_far, totals = carry
        gives = jnp.where(ginfo[i, 8:16, :] == 0, 1, 0)
        ichip = lax.div(i, 2)
        iline = lax.rem(ichip, 2)
        ilow = lax.div(ichip, 2) < reach
        here = jnp.where((iline == line) & (ilow == at.low), 1, 0)
        there = jnp.where((iline == line) & (ilow != at.low), 1, 0)
        ahead_me = ahead_me + gives * (here * jnp.where(i < me, 1, 0))
        ahead_sib = ahead_sib + gives * (here * jnp.where(i < at.sibling, 1, 0))
        ahead_far = ahead_far + gives * (there * jnp.where(i < partner, 1, 0))
        totals = tuple(
            t + gives * jnp.where((iline == b % 2) & (jnp.where(ilow, 1, 0) == b // 2), 1, 0)
            for b, t in enumerate(totals))
        return ahead_me, ahead_sib, ahead_far, totals

    zero = jnp.zeros((8, TILE), jnp.int32)
    ahead_me, ahead_sib, ahead_far, totals = lax.fori_loop(
        0, count, tally, (zero, zero, zero, (zero,) * 4))
    for slot, (who, ahead) in enumerate(((me, ahead_me), (at.sibling, ahead_sib), (partner, ahead_far))):
        plan[slot * 8:slot * 8 + 8, :] = jnp.where(ginfo[who, 8:16, :] == 0, ahead, -1)
    top[...] = jnp.maximum(jnp.maximum(totals[0], totals[1]), jnp.maximum(totals[2], totals[3]))

    scale = HEAD_WIDTH ** -0.5

    def attend(h):
        def half(k, c):
            keys = kv[h, pl.ds(core, NEAR_TILES), :, 0:HEAD_WIDTH].reshape(NEAR_TILES * TILE, HEAD_WIDTH)
            vals = kv[h, pl.ds(core, NEAR_TILES), :, HEAD_WIDTH:].reshape(NEAR_TILES * TILE, HEAD_WIDTH)
            for j in range(HALF_HEADS):
                at_col = pl.multiple_of((h * GROUP_HEADS + k * HALF_HEADS + j) * HEAD_WIDTH, HEAD_WIDTH)
                s = lax.dot_general(q[:, pl.ds(at_col, HEAD_WIDTH)], keys, (((1,), (1,)), ((), ())),
                                    preferred_element_type=jnp.float32)
                s = s * scale + bias[...]
                e = jnp.exp(s - jnp.max(s, axis=1, keepdims=True))
                total = jnp.sum(e, axis=1, keepdims=True)
                mixed = jnp.dot(e.astype(jnp.bfloat16), vals, preferred_element_type=jnp.float32)
                o[h, k, :, j * HEAD_WIDTH:(j + 1) * HEAD_WIDTH] = (mixed / total).astype(jnp.bfloat16)
            return c
        lax.fori_loop(0, 2, half, 0)

    def relay_two(h):
        @pl.when(chip >= 2)
        def _():
            arrived(h, core)

            @pl.when(line == 1)
            def _():
                relay_one(h).start()

            @pl.when(core == 1)
            def _():
                sib_two(h).start()

    def relay_sib(h):
        @pl.when(chip >= 1)
        def _():
            arrived(h, 2 + core)
            sib_one(h).start()

    def compute(h):
        @pl.when(chip >= 1)
        def _():
            arrived(h, 3 - core)

        @pl.when((chip >= 2) & (core == 0))
        def _():
            arrived(h, 1)

        @pl.when(core == 1)
        def _():
            arrived(h, 4)

        local(h).wait()
        q_copy(h).wait()
        attend(h)
        bus.share(h).start()

    def step(u):
        for lag, stage in ((0, relay_two), (1, relay_sib), (2, compute), (3, bus.inject), (3 + at.lag, bus.forward)):
            h = u - lag

            @pl.when((h >= 0) & (h < KEY_VALUE_HEADS))
            def _():
                stage(h)

    each(KEY_VALUE_HEADS + 3 + at.longest, step)

    for by in range(1, groups):
        top_copy(by).start()

    def drain(h):
        bus.drain(h)

        @pl.when(has_two_up)
        def _():
            up_two(h).wait_send()

        @pl.when((line == 0) | (chip >= 2))
        def _():
            up_one(h).wait_send()

        @pl.when(core == 0)
        def _():
            sib_own(h).wait_send()

        @pl.when(chip >= 1)
        def _():
            sib_one(h).wait_send()

        @pl.when((chip >= 2) & (core == 1))
        def _():
            sib_two(h).wait_send()

    heads(drain)
    peers(lambda p: info_to(p).wait_send())
    for by in range(1, groups):
        top_copy(by).wait()
    most = top[...]
    for by in range(1, groups):
        most = jnp.maximum(most, topin[by])
    top[...] = most


def round_kernel(count, o, sib, plan, turn, far, farsib, injin, inj, bus_s, bus_r):
    at = Place(count)
    barrier = pltpu.get_barrier_semaphore()
    for seq, there in ((at.sibling, None), (at.inner, None), (at.outer, at.rim > 0)):
        def greet():
            pl.semaphore_signal(barrier, inc=1, device_id={"seq": seq}, device_id_type=MESH)
        if there is None:
            greet()
        else:
            pl.when(there)(greet)
    pl.semaphore_wait(barrier, jnp.where(at.rim > 0, 3, 2))

    bus = Bus(at, o, plan, sib, far, farsib, injin, inj, bus_s, bus_r, lambda: turn[0:1, :])

    def step(u, c):
        for lag, stage in ((0, functools.partial(bus.inject, shared=False)), (at.lag, bus.forward)):
            h = u - lag

            @pl.when((h >= 0) & (h < KEY_VALUE_HEADS))
            def _():
                stage(h)
        return c

    lax.fori_loop(0, KEY_VALUE_HEADS + at.longest, step, 0)

    def drain(h, c):
        bus.drain(h, shared=False)
        return c

    lax.fori_loop(0, KEY_VALUE_HEADS, drain, 0)


def place_kernel(tiles, valid, o, far, farsib, out, blank, sems):
    me = lax.axis_index("seq")
    core = lax.rem(me, 2)
    slots = out.shape[0] // TILE
    blank[...] = jnp.zeros_like(blank)

    def parts(h):
        cols = [pl.ds(pl.multiple_of((2 * h + k) * HALF_COLS, HALF_COLS), HALF_COLS) for k in (0, 1)]
        here = pl.ds(pl.multiple_of((2 * h + core) * HALF_COLS, HALF_COLS), HALF_COLS)
        there = pl.ds(pl.multiple_of((2 * h + 1 - core) * HALF_COLS, HALF_COLS), HALF_COLS)
        mine = [(o.at[h, 0], cols[0]), (o.at[h, 1], cols[1])]
        theirs = [(far.at[h], here), (farsib.at[h], there)]
        none = [(blank, c) for c in cols]
        return mine, theirs, none

    def run(h, c, go):
        for s in range(slots):
            live = s < valid[0]
            own = live & (tiles[0, s] == me)
            cases = (own, live & jnp.logical_not(own), jnp.logical_not(live))
            for case, pieces in zip(cases, parts(h)):
                @pl.when(case)
                def _():
                    for k, (src, cols) in enumerate(pieces):
                        go(pltpu.make_async_copy(
                            src, out.at[pl.ds(s * TILE, TILE), cols], sems.at[h, s, k]))
        return c

    lax.fori_loop(0, KEY_VALUE_HEADS, functools.partial(run, go=lambda x: x.start()), 0)
    lax.fori_loop(0, KEY_VALUE_HEADS, functools.partial(run, go=lambda x: x.wait()), 0)


def local(groups, count, queries, keyvalue, doc_ids, owner_tiles, tile_counts):
    width = queries.shape[1]
    slots = owner_tiles.shape[1]
    marks = doc_ids + 1
    info = jnp.concatenate([
        jnp.broadcast_to(marks[None, :], (8, TILE)),
        jnp.broadcast_to(tile_counts[:, None], (8, TILE))], axis=0)
    qmark = jnp.broadcast_to(marks[:, None], (TILE, TILE))
    H = KEY_VALUE_HEADS
    bf, i32 = jnp.bfloat16, jnp.int32
    part = (H, TILE, HALF_COLS)
    dma = pltpu.SemaphoreType.DMA
    o, sib, far, farsib, plan, top = pl.pallas_call(
        functools.partial(main_kernel, groups, count),
        out_shape=[
            jax.ShapeDtypeStruct((H, 2, TILE, HALF_COLS), bf),
            jax.ShapeDtypeStruct(part, bf),
            jax.ShapeDtypeStruct(part, bf),
            jax.ShapeDtypeStruct(part, bf),
            jax.ShapeDtypeStruct((24, TILE), i32),
            jax.ShapeDtypeStruct((8, TILE), i32),
        ],
        in_specs=[pl.BlockSpec(memory_space=pltpu.HBM)] * 2 + [VMEM] * 2,
        out_specs=[VMEM] * 6,
        scratch_shapes=[
            pltpu.VMEM(queries.shape, bf),
            pltpu.VMEM((H, 6, TILE, KV_COLS), bf),
            pltpu.VMEM((count, 16, TILE), i32),
            pltpu.VMEM((TILE, NEAR_TILES * TILE), jnp.float32),
            pltpu.VMEM(part, bf),
            pltpu.VMEM(part, bf),
            pltpu.VMEM((groups, 8, TILE), i32),
            dma((H,)),
            dma((H,)),
            dma((count,)),
            dma((count,)),
            dma((groups,)),
            dma((groups,)),
            dma((5, H)),
            dma((H, 6)),
            dma((4, H)),
            dma((4, H)),
        ],
        compiler_params=pltpu.CompilerParams(
            collective_id=0, has_side_effects=True, vmem_limit_bytes=40 << 20),
    )(keyvalue, queries, qmark, info)

    def again(turn, held):
        turns = jnp.full((8, TILE), turn, i32)
        new = pl.pallas_call(
            functools.partial(round_kernel, count),
            out_shape=[jax.ShapeDtypeStruct(part, bf)] * 2,
            in_specs=[VMEM] * 4,
            out_specs=[VMEM] * 2,
            scratch_shapes=[
                pltpu.VMEM(part, bf),
                pltpu.VMEM(part, bf),
                dma((4, H)),
                dma((4, H)),
            ],
            compiler_params=pltpu.CompilerParams(
                collective_id=1, has_side_effects=True, vmem_limit_bytes=24 << 20),
        )(o, sib, plan, turns)
        here = plan[16, 0] == turn
        return tuple(jnp.where(here, n, h) for n, h in zip(new, held))

    far, farsib = lax.fori_loop(1, top[0, 0], again, (far, farsib))

    return pl.pallas_call(
        place_kernel,
        out_shape=jax.ShapeDtypeStruct((slots * TILE, width), bf),
        in_specs=[pl.BlockSpec(memory_space=pltpu.SMEM)] * 2 + [VMEM] * 3,
        out_specs=pl.BlockSpec(memory_space=pl.ANY),
        scratch_shapes=[pltpu.VMEM((TILE, HALF_COLS), bf), dma((H, slots, 2))],
        compiler_params=pltpu.CompilerParams(vmem_limit_bytes=16 << 20),
    )(owner_tiles, tile_counts, o, far, farsib)


def solution(mesh):
    spread = P(("groups", "seq"))
    rows = P(("groups", "seq"), None)
    return jax.shard_map(
        functools.partial(local, mesh.shape["groups"], mesh.shape["seq"]), mesh=mesh,
        in_specs=(rows, rows, spread, rows, spread), out_specs=rows, check_vma=False)
```

```python
import functools

import jax
import jax.numpy as jnp
from jax import lax
from jax.experimental import pallas as pl
from jax.experimental.pallas import tpu as pltpu
from jax.sharding import PartitionSpec as P

QUERY_HEADS = 64
KEY_VALUE_HEADS = 8
HEAD_WIDTH = 128
TILE = 128
DOCUMENT_LIMIT = 512

MESH = pl.DeviceIdType.MESH
NEAR_TILES = DOCUMENT_LIMIT // TILE + 1
GROUP_HEADS = QUERY_HEADS // KEY_VALUE_HEADS
SPLIT = 2
UNITS = KEY_VALUE_HEADS * SPLIT
UNIT_HEADS = GROUP_HEADS // SPLIT
UNIT_COLS = UNIT_HEADS * HEAD_WIDTH
GROUP_COLS = SPLIT * UNIT_COLS
HALF_ROWS = TILE // 2
KV_COLS = 2 * HEAD_WIDTH
MASKED = -1e30
VMEM = pl.BlockSpec(memory_space=pltpu.VMEM)


class Place:
    def __init__(self, count):
        self.me = me = lax.axis_index("seq")
        self.core = lax.rem(me, 2)
        self.chip = chip = lax.div(me, 2)
        self.line = lax.rem(chip, 2)
        self.depth = lax.div(chip, 2)
        self.depths = count // 4
        reach = self.depths // 2
        self.low = self.depth < reach
        step = jnp.where(self.low, 4, -4)
        self.inner = me + step
        self.outer = me - step
        self.rim = jnp.where(self.low, self.depth, self.depths - 1 - self.depth)
        self.crossing = self.rim == reach - 1
        self.lag = 3 * (2 * (reach - 1 - self.rim) + 1)
        self.longest = 3 * (2 * reach - 1)
        self.sibling = me + 1 - 2 * self.core


def remote(src, dst, send_sem, recv_sem, seq):
    return pltpu.make_async_remote_copy(
        src_ref=src, dst_ref=dst, send_sem=send_sem, recv_sem=recv_sem,
        device_id={"seq": seq}, device_id_type=MESH)


class Bus:
    def __init__(self, at, o, plan, sib, far, farsib, injin, inj, sends, recvs, turn):
        self.__dict__.update(locals())

    def share(self, h):
        return remote(self.o.at[h, 1 - self.at.core], self.sib.at[h],
                      self.sends.at[0, h], self.recvs.at[0, h], self.at.sibling)

    def inward(self, h):
        return remote(self.inj.at[h], self.injin.at[h],
                      self.sends.at[1, h], self.recvs.at[1, h], self.at.inner)

    def across(self, h):
        return remote(self.inj.at[h], self.far.at[h],
                      self.sends.at[1, h], self.recvs.at[2, h], self.at.inner)

    def outward(self, h):
        return remote(self.far.at[h], self.far.at[h],
                      self.sends.at[2, h], self.recvs.at[2, h], self.at.outer)

    def hand(self, h):
        return remote(self.far.at[h], self.farsib.at[h],
                      self.sends.at[3, h], self.recvs.at[3, h], self.at.sibling)

    def compose(self, h, below):
        turn = self.turn()
        own_here = jnp.broadcast_to(self.plan[0:1, :] == turn, (HALF_ROWS, TILE))
        sib_here = jnp.broadcast_to(self.plan[8:9, :] == turn, (HALF_ROWS, TILE))
        for c in range(0, UNIT_COLS, TILE):
            cols = slice(c, c + TILE)
            own = self.o[h, self.at.core, :, cols].astype(jnp.float32)
            new = self.sib[h, :, cols].astype(jnp.float32)
            if below:
                new = jnp.where(sib_here, new, self.injin[h, :, cols].astype(jnp.float32))
            self.inj[h, :, cols] = jnp.where(own_here, own, new).astype(jnp.bfloat16)

    def inject(self, h, shared=True):
        if shared:
            self.share(h).wait_recv()

        @pl.when(self.at.rim == 0)
        def _():
            self.compose(h, False)

        @pl.when(self.at.rim > 0)
        def _():
            self.inward(h).wait_recv()
            self.compose(h, True)

        @pl.when(self.at.crossing)
        def _():
            self.across(h).start()

        @pl.when(jnp.logical_not(self.at.crossing))
        def _():
            self.inward(h).start()

    def forward(self, h):
        self.outward(h).wait_recv()

        @pl.when(self.at.rim > 0)
        def _():
            self.outward(h).start()

        self.hand(h).start()

    def drain(self, h, shared=True):
        if shared:
            self.share(h).wait_send()
        self.inward(h).wait_send()

        @pl.when(self.at.rim > 0)
        def _():
            self.outward(h).wait_send()

        self.hand(h).wait()


def main_kernel(groups, count, kv_hbm, q_hbm, qmark, info,
                o, sib, far, farsib, plan, top,
                q, kv, ginfo, bias, injin, inj, topin,
                ql, kvl, info_s, info_r, top_s, top_r, kv_s, kv_r, bus_s, bus_r):
    at = Place(count)
    me, core, chip, line = at.me, at.core, at.chip, at.line
    group = lax.axis_index("groups")
    chips = count // 2
    bus = Bus(at, o, plan, sib, far, farsib, injin, inj, bus_s, bus_r, lambda: 0)

    def own(h):
        return kv_hbm.at[:, pl.ds(pl.multiple_of(h * KV_COLS, KV_COLS), KV_COLS)]

    def local(h):
        return pltpu.make_async_copy(own(h), kv.at[h, 4 + core], kvl.at[h])

    def q_copy(h):
        cols = pl.ds(pl.multiple_of(h * GROUP_COLS, GROUP_COLS), GROUP_COLS)
        return pltpu.make_async_copy(q_hbm.at[:, cols], q.at[:, cols], ql.at[h])

    def up_two(h):
        return remote(own(h), kv.at[h, core], kv_s.at[0, h], kv_r.at[h, core], me + 4)

    def up_one(h):
        return remote(own(h), kv.at[h, 2 + core], kv_s.at[1, h], kv_r.at[h, 2 + core], me + 2)

    def relay_one(h):
        return remote(kv.at[h, core], kv.at[h, 2 + core], kv_s.at[1, h], kv_r.at[h, 2 + core], me - 2)

    def sib_own(h):
        return remote(own(h), kv.at[h, 4], kv_s.at[2, h], kv_r.at[h, 4], at.sibling)

    def sib_one(h):
        return remote(kv.at[h, 2 + core], kv.at[h, 2 + core], kv_s.at[3, h],
                      kv_r.at[h, 2 + core], at.sibling)

    def sib_two(h):
        return remote(kv.at[h, 1], kv.at[h, 1], kv_s.at[4, h], kv_r.at[h, 1], at.sibling)

    def arrived(h, slot):
        remote(kv.at[h, slot], kv.at[h, slot], kv_s.at[0, h], kv_r.at[h, slot],
               at.sibling).wait_recv()

    def info_to(peer):
        return remote(info, ginfo.at[me], info_s.at[peer], info_r.at[me], peer)

    def info_from(peer):
        return remote(info, ginfo.at[peer], info_s.at[peer], info_r.at[peer], peer)

    def top_copy(by):
        to = lax.rem(group + by, groups)
        return pltpu.make_async_remote_copy(
            src_ref=top, dst_ref=topin.at[by], send_sem=top_s.at[by], recv_sem=top_r.at[by],
            device_id={"groups": to}, device_id_type=MESH)

    def each(n, body):
        lax.fori_loop(0, n, lambda i, c: (body(i), c)[1], 0)

    def peers(body):
        def one(i):
            body(lax.rem(me + 1 + i, count))
        each(count - 1, one)

    heads = functools.partial(each, KEY_VALUE_HEADS)

    heads(lambda h: local(h).start())
    heads(lambda h: q_copy(h).start())
    barrier = pltpu.get_barrier_semaphore()
    peers(lambda p: pl.semaphore_signal(barrier, inc=1, device_id={"seq": p}, device_id_type=MESH))
    for by in range(1, groups):
        pl.semaphore_signal(barrier, inc=1, device_id={"groups": lax.rem(group + by, groups)},
                            device_id_type=MESH)
    pl.semaphore_wait(barrier, count - 1 + groups - 1)

    has_two_up = chip + 2 < chips

    def launch(h):
        @pl.when(has_two_up)
        def _():
            up_two(h).start()

        @pl.when(line == 0)
        def _():
            up_one(h).start()

        @pl.when(core == 0)
        def _():
            sib_own(h).start()

    launch(0)
    peers(lambda p: info_to(p).start())
    each(KEY_VALUE_HEADS - 1, lambda h: launch(h + 1))

    blank = jnp.zeros((TILE, KV_COLS), jnp.bfloat16)

    @pl.when(chip < 2)
    def _():
        def clear(h):
            kv[h, 0] = blank
            kv[h, 1] = blank
        heads(clear)

    @pl.when(chip < 1)
    def _():
        def clear(h):
            kv[h, 2] = blank
            kv[h, 3] = blank
        heads(clear)

    def prepare():
        ginfo[me] = info[...]
        peers(lambda p: info_from(p).wait_recv())

        rows = lax.broadcasted_iota(jnp.int32, (TILE, TILE), 0)
        cols = lax.broadcasted_iota(jnp.int32, (TILE, TILE), 1)
        for w in range(NEAR_TILES):
            tile = me - (NEAR_TILES - 1) + w
            marks = ginfo[jnp.maximum(tile, 0), 0:1, :] - jnp.where(tile < 0, 1 << 20, 0)
            allowed = qmark[...] == jnp.broadcast_to(marks, (TILE, TILE))
            if w == NEAR_TILES - 1:
                allowed = allowed & (cols <= rows)
            bias[:, w * TILE:(w + 1) * TILE] = jnp.where(allowed, 0.0, MASKED).astype(jnp.float32)

        partner = lax.rem(me + count // 2, count)
        reach = at.depths // 2

        def tally(i, carry):
            ahead_me, ahead_sib, ahead_far, totals = carry
            gives = jnp.where(ginfo[i, 8:16, :] == 0, 1, 0)
            ichip = lax.div(i, 2)
            iline = lax.rem(ichip, 2)
            ilow = lax.div(ichip, 2) < reach
            here = jnp.where((iline == line) & (ilow == at.low), 1, 0)
            there = jnp.where((iline == line) & (ilow != at.low), 1, 0)
            ahead_me = ahead_me + gives * (here * jnp.where(i < me, 1, 0))
            ahead_sib = ahead_sib + gives * (here * jnp.where(i < at.sibling, 1, 0))
            ahead_far = ahead_far + gives * (there * jnp.where(i < partner, 1, 0))
            totals = tuple(
                t + gives * jnp.where((iline == b % 2) & (jnp.where(ilow, 1, 0) == b // 2), 1, 0)
                for b, t in enumerate(totals))
            return ahead_me, ahead_sib, ahead_far, totals

        zero = jnp.zeros((8, TILE), jnp.int32)
        ahead_me, ahead_sib, ahead_far, totals = lax.fori_loop(
            0, count, tally, (zero, zero, zero, (zero,) * 4))
        for slot, (who, ahead) in enumerate(((me, ahead_me), (at.sibling, ahead_sib), (partner, ahead_far))):
            plan[slot * 8:slot * 8 + 8, :] = jnp.where(ginfo[who, 8:16, :] == 0, ahead, -1)
        top[...] = jnp.maximum(jnp.maximum(totals[0], totals[1]), jnp.maximum(totals[2], totals[3]))

    scale = HEAD_WIDTH ** -0.5

    def attend(b, h):
        keys = kv[h, pl.ds(core, NEAR_TILES), :, 0:HEAD_WIDTH].reshape(NEAR_TILES * TILE, HEAD_WIDTH)
        vals = kv[h, pl.ds(core, NEAR_TILES), :, HEAD_WIDTH:].reshape(NEAR_TILES * TILE, HEAD_WIDTH)
        for j in range(UNIT_HEADS):
            at_col = pl.multiple_of((b * UNIT_HEADS + j) * HEAD_WIDTH, HEAD_WIDTH)
            s = lax.dot_general(q[:, pl.ds(at_col, HEAD_WIDTH)], keys, (((1,), (1,)), ((), ())),
                                preferred_element_type=jnp.float32)
            s = s * scale + bias[...]
            e = jnp.exp(s - jnp.max(s, axis=1, keepdims=True))
            total = jnp.sum(e, axis=1, keepdims=True)
            mixed = jnp.dot(e.astype(jnp.bfloat16), vals, preferred_element_type=jnp.float32)
            mixed = (mixed / total).astype(jnp.bfloat16)
            for k in (0, 1):
                o[b, k, :, j * HEAD_WIDTH:(j + 1) * HEAD_WIDTH] = mixed[k * HALF_ROWS:(k + 1) * HALF_ROWS]

    def relay_two(h):
        @pl.when(chip >= 2)
        def _():
            arrived(h, core)

            @pl.when(line == 1)
            def _():
                relay_one(h).start()

            @pl.when(core == 1)
            def _():
                sib_two(h).start()

    def relay_sib(h):
        @pl.when(chip >= 1)
        def _():
            arrived(h, 2 + core)
            sib_one(h).start()

    def ready(h):
        @pl.when(chip >= 1)
        def _():
            arrived(h, 3 - core)

        @pl.when((chip >= 2) & (core == 0))
        def _():
            arrived(h, 1)

        @pl.when(core == 1)
        def _():
            arrived(h, 4)

        local(h).wait()
        q_copy(h).wait()

    def compute(b):
        h = lax.div(b, SPLIT)

        @pl.when(lax.rem(b, SPLIT) == 0)
        def _():
            ready(h)

        attend(b, h)
        bus.share(b).start()

    def relays(u):
        for lag, stage in ((0, relay_two), (1, relay_sib)):
            h = lax.div(u - lag, SPLIT)

            @pl.when((u >= lag) & (lax.rem(u - lag, SPLIT) == 0) & (h < KEY_VALUE_HEADS))
            def _():
                stage(h)

    each(2, relays)
    prepare()

    def step(i):
        u = i + 2
        relays(u)
        for lag, stage in ((2, compute), (3, bus.inject), (3 + at.lag, bus.forward)):
            b = u - lag

            @pl.when((b >= 0) & (b < UNITS))
            def _():
                stage(b)

    each(UNITS + 1 + at.longest, step)

    for by in range(1, groups):
        top_copy(by).start()

    each(UNITS, bus.drain)

    def drain(h):
        @pl.when(has_two_up)
        def _():
            up_two(h).wait_send()

        @pl.when((line == 0) | (chip >= 2))
        def _():
            up_one(h).wait_send()

        @pl.when(core == 0)
        def _():
            sib_own(h).wait_send()

        @pl.when(chip >= 1)
        def _():
            sib_one(h).wait_send()

        @pl.when((chip >= 2) & (core == 1))
        def _():
            sib_two(h).wait_send()

    heads(drain)
    peers(lambda p: info_to(p).wait_send())
    for by in range(1, groups):
        top_copy(by).wait()
    most = top[...]
    for by in range(1, groups):
        most = jnp.maximum(most, topin[by])
    top[...] = most


def round_kernel(count, o, sib, plan, turn, far, farsib, injin, inj, bus_s, bus_r):
    at = Place(count)
    barrier = pltpu.get_barrier_semaphore()
    for seq, there in ((at.sibling, None), (at.inner, None), (at.outer, at.rim > 0)):
        def greet():
            pl.semaphore_signal(barrier, inc=1, device_id={"seq": seq}, device_id_type=MESH)
        if there is None:
            greet()
        else:
            pl.when(there)(greet)
    pl.semaphore_wait(barrier, jnp.where(at.rim > 0, 3, 2))

    bus = Bus(at, o, plan, sib, far, farsib, injin, inj, bus_s, bus_r, lambda: turn[0:1, :])

    def step(u, c):
        for lag, stage in ((0, functools.partial(bus.inject, shared=False)), (at.lag, bus.forward)):
            h = u - lag

            @pl.when((h >= 0) & (h < UNITS))
            def _():
                stage(h)
        return c

    lax.fori_loop(0, UNITS + at.longest, step, 0)

    def drain(h, c):
        bus.drain(h, shared=False)
        return c

    lax.fori_loop(0, UNITS, drain, 0)


def place_kernel(tiles, valid, o, far, farsib, out, blank, sems):
    me = lax.axis_index("seq")
    core = lax.rem(me, 2)
    slots = out.shape[0] // TILE
    blank[...] = jnp.zeros_like(blank)

    def run(b, c, go):
        cols = pl.ds(pl.multiple_of(b * UNIT_COLS, UNIT_COLS), UNIT_COLS)
        mine = ((o.at[b, 0], 0), (o.at[b, 1], HALF_ROWS))
        theirs = ((far.at[b], core * HALF_ROWS), (farsib.at[b], (1 - core) * HALF_ROWS))
        none = ((blank, 0), (blank, HALF_ROWS))
        for s in range(slots):
            live = s < valid[0]
            own = live & (tiles[0, s] == me)
            for case, pieces in ((own, mine), (live & jnp.logical_not(own), theirs),
                                 (jnp.logical_not(live), none)):
                @pl.when(case)
                def _():
                    for k, (src, row) in enumerate(pieces):
                        rows = pl.ds(pl.multiple_of(s * TILE + row, HALF_ROWS), HALF_ROWS)
                        go(pltpu.make_async_copy(src, out.at[rows, cols], sems.at[b, s, k]))
        return c

    lax.fori_loop(0, UNITS, functools.partial(run, go=lambda x: x.start()), 0)
    lax.fori_loop(0, UNITS, functools.partial(run, go=lambda x: x.wait()), 0)


def local(groups, count, queries, keyvalue, doc_ids, owner_tiles, tile_counts):
    width = queries.shape[1]
    slots = owner_tiles.shape[1]
    marks = doc_ids + 1
    info = jnp.concatenate([
        jnp.broadcast_to(marks[None, :], (8, TILE)),
        jnp.broadcast_to(tile_counts[:, None], (8, TILE))], axis=0)
    qmark = jnp.broadcast_to(marks[:, None], (TILE, TILE))
    H = KEY_VALUE_HEADS
    bf, i32 = jnp.bfloat16, jnp.int32
    part = (UNITS, HALF_ROWS, UNIT_COLS)
    dma = pltpu.SemaphoreType.DMA
    o, sib, far, farsib, plan, top = pl.pallas_call(
        functools.partial(main_kernel, groups, count),
        out_shape=[
            jax.ShapeDtypeStruct((UNITS, 2, HALF_ROWS, UNIT_COLS), bf),
            jax.ShapeDtypeStruct(part, bf),
            jax.ShapeDtypeStruct(part, bf),
            jax.ShapeDtypeStruct(part, bf),
            jax.ShapeDtypeStruct((24, TILE), i32),
            jax.ShapeDtypeStruct((8, TILE), i32),
        ],
        in_specs=[pl.BlockSpec(memory_space=pltpu.HBM)] * 2 + [VMEM] * 2,
        out_specs=[VMEM] * 6,
        scratch_shapes=[
            pltpu.VMEM(queries.shape, bf),
            pltpu.VMEM((H, 6, TILE, KV_COLS), bf),
            pltpu.VMEM((count, 16, TILE), i32),
            pltpu.VMEM((TILE, NEAR_TILES * TILE), jnp.float32),
            pltpu.VMEM(part, bf),
            pltpu.VMEM(part, bf),
            pltpu.VMEM((groups, 8, TILE), i32),
            dma((H,)),
            dma((H,)),
            dma((count,)),
            dma((count,)),
            dma((groups,)),
            dma((groups,)),
            dma((5, H)),
            dma((H, 6)),
            dma((4, UNITS)),
            dma((4, UNITS)),
        ],
        compiler_params=pltpu.CompilerParams(
            collective_id=0, has_side_effects=True, vmem_limit_bytes=56 << 20),
    )(keyvalue, queries, qmark, info)

    def again(turn, held):
        turns = jnp.full((8, TILE), turn, i32)
        new = pl.pallas_call(
            functools.partial(round_kernel, count),
            out_shape=[jax.ShapeDtypeStruct(part, bf)] * 2,
            in_specs=[VMEM] * 4,
            out_specs=[VMEM] * 2,
            scratch_shapes=[
                pltpu.VMEM(part, bf),
                pltpu.VMEM(part, bf),
                dma((4, UNITS)),
                dma((4, UNITS)),
            ],
            compiler_params=pltpu.CompilerParams(
                collective_id=1, has_side_effects=True, vmem_limit_bytes=24 << 20),
        )(o, sib, plan, turns)
        here = plan[16, 0] == turn
        return tuple(jnp.where(here, n, h) for n, h in zip(new, held))

    far, farsib = lax.fori_loop(1, top[0, 0], again, (far, farsib))

    return pl.pallas_call(
        place_kernel,
        out_shape=jax.ShapeDtypeStruct((slots * TILE, width), bf),
        in_specs=[pl.BlockSpec(memory_space=pltpu.SMEM)] * 2 + [VMEM] * 3,
        out_specs=pl.BlockSpec(memory_space=pl.ANY),
        scratch_shapes=[pltpu.VMEM((HALF_ROWS, UNIT_COLS), bf), dma((UNITS, slots, 2))],
        compiler_params=pltpu.CompilerParams(vmem_limit_bytes=16 << 20),
    )(owner_tiles, tile_counts, o, far, farsib)


def solution(mesh):
    spread = P(("groups", "seq"))
    rows = P(("groups", "seq"), None)
    return jax.shard_map(
        functools.partial(local, mesh.shape["groups"], mesh.shape["seq"]), mesh=mesh,
        in_specs=(rows, rows, spread, rows, spread), out_specs=rows, check_vma=False)
```
